32 devices in a mesh: pts: 4 (over x, core), atom: 8 (over z, y).
Axes of the slice: x: 2, y: 2, z: 4, core: 2. Of those that a mesh axis runs over, the one named last changes fastest.
Arguments:
- points: bfloat16 [131072, 256], P(('pts', 'atom')), may hold values from -6 to 6
- atoms: bfloat16 [4096, 256], P('atom'), may hold values from -6 to 6
- kept: int32 [1024, 4], P(('pts', 'atom')), may hold values from 0 to 11, as said below
- point_logw: float32 [131072], P(('pts', 'atom')), may hold values from -4 to 4
- atom_logw: float32 [4096], P('atom'), may hold values from -4 to 4
- epsilons: float32 [2], replicated, may hold values from 0.004 to 0.008
- relaxation: float32 [1], replicated, may hold values from 0.02 to 0.2
Outputs:
- point_potential: float32 [131072], P(('pts', 'atom'))
- atom_potential: float32 [4096], P('atom')
- point_log_mass: float32 [131072], P(('pts', 'atom'))
The draws below stay inside these ranges and needn't reach their ends.
Inputs may be any that keep to these rules, and one draw needn't show every extreme that they name: `kept`: the entries of one row are distinct.
All inputs are finite; a program needn't handle non-finite values.
Results may differ from the reference program's by a relative error of at most 0.0003.
Values may be sent and summed in bfloat16 or wider, within the bound.
A program may use at most 64 MiB of HBM per device.

```python
import math
import jax
import jax.numpy as jnp
from jax import lax

D = 256
PTS_DEV = 4096
ATOM_DEV = 512
KEEP = 4
ITERS = 2
PANELS = 8
NP = 131072
NA = 4096


def shared_kept(key):
    per_panel = ATOM_DEV // 128
    per_device = PTS_DEV // 128
    window_blocks = 3 * per_panel
    block_count = NP // 128
    block_index = jnp.arange(block_count, dtype=jnp.int32)
    leading = per_panel + block_index % per_device % per_panel
    columns = jnp.arange(window_blocks, dtype=jnp.int32)
    scores = jax.random.randint(jax.random.fold_in(key, 12), (block_count, window_blocks), 0, 4096, dtype=jnp.int32) * window_blocks + columns[None]
    scores = jnp.where(columns[None] == leading[:, None], -1, scores)
    _, others = lax.top_k(scores, KEEP - 1)
    return jnp.concatenate([leading[:, None], others.astype(jnp.int32)], axis=1)


def shared_atoms(key):
    base = jax.random.normal(jax.random.fold_in(key, 11), (NA, D), jnp.float32)
    return jnp.clip(base, -5.9, 5.9)


def draw_atoms(key, part):
    return shared_atoms(key).astype(jnp.bfloat16)


def draw_kept(key, part):
    return shared_kept(key)


def draw_points(key, part):
    base = jax.random.normal(jax.random.fold_in(key, 13), (NP, D), jnp.float32)
    return jnp.clip(base, -5.9, 5.9).astype(jnp.bfloat16)


def level_of(key, dims, split, low, high):
    level, own = 1.0, jax.random.fold_in(key, 6)
    for axis_at, blocks in split:
        steps = jnp.exp(jax.random.uniform(jax.random.fold_in(own, axis_at), (blocks,), jnp.float32, low / len(split), high / len(split)))
        level = level * jnp.repeat(steps, dims[axis_at] // blocks).reshape([-1 if axis == axis_at else 1 for axis in range(len(dims))])
    return level


def normal_values(rng, extent, scale, reach, pieces=(), kind=jnp.bfloat16):
    drawn = jax.random.normal(rng, extent, jnp.float32) * scale
    if len(pieces) > 0:
        drawn = level_of(rng, extent, pieces, -0.22, 0.18) * drawn
    return jnp.clip(drawn, min=-reach, max=reach).astype(kind)


def setup_inputs(seed: int = 0) -> dict:
    key_of = jax.random.split(jax.random.key(seed), 8)
    return {
        "points": draw_points(jax.random.fold_in(key_of[7], 71), 0),
        "atoms": draw_atoms(jax.random.fold_in(key_of[7], 71), 0),
        "kept": draw_kept(jax.random.fold_in(key_of[7], 71), 0),
        "point_logw": normal_values(key_of[3], (NP,), 1.0, 4.0, ((0, 32),), jnp.float32),
        "atom_logw": normal_values(key_of[4], (NA,), 1.0, 4.0, ((0, 8),), jnp.float32),
        "epsilons": jnp.clip(jnp.exp(jax.random.uniform(key_of[5], (ITERS,), jnp.float32, math.log(0.004), math.log(0.008))), 0.004, 0.008),
        "relaxation": jnp.clip(jnp.exp(jax.random.uniform(key_of[6], (1,), jnp.float32, math.log(0.02), math.log(0.2))), 0.02, 0.2),
    }


lowest = -1.0e30


def merge_terms(earlier, later):
    highest = jnp.maximum(earlier[0], later[0])
    return (highest, earlier[1] * jnp.exp(earlier[0] - highest) + later[1] * jnp.exp(later[0] - highest))


def reference(points, atoms, kept, point_logw, atom_logw, epsilons, relaxation):
    per_device = PTS_DEV // 128
    per_panel = ATOM_DEV // 128
    point_blocks = points.shape[0] // 128
    atom_blocks = atoms.shape[0] // 128
    block_index = jnp.arange(point_blocks, dtype=jnp.int32)
    panel_index = (block_index // per_device) % PANELS
    global_ids = ((panel_index[:, None] + kept // per_panel - 1 + PANELS) % PANELS) * per_panel + kept % per_panel
    global_ids = global_ids.astype(jnp.int32)
    point_tiles = points.reshape(point_blocks, 128, D)
    atom_tiles = atoms.reshape(atom_blocks, 128, D)
    sq_points = jnp.sum(jnp.square(point_tiles.astype(jnp.float32)), axis=2)
    sq_atoms = jnp.sum(jnp.square(atom_tiles.astype(jnp.float32)), axis=2)
    logw_points = point_logw.reshape(point_blocks, 128)
    logw_atoms = atom_logw.reshape(atom_blocks, 128)

    def tile_costs(point_tile, sq_tile, chosen_ids):
        chosen = atom_tiles[chosen_ids].astype(jnp.float32)
        products = jnp.einsum("pd,kad->pka", point_tile.astype(jnp.float32), chosen, precision=lax.Precision.HIGHEST)
        return (sq_tile[:, None, None] + sq_atoms[chosen_ids][None] - 2.0 * products) / (2.0 * D)

    def point_sums(atom_pot, epsilon):
        def one_block(inputs):
            point_tile, sq_tile, chosen_ids = inputs
            tile_cost = tile_costs(point_tile, sq_tile, chosen_ids)
            scores = logw_atoms[chosen_ids][None] + (atom_pot[chosen_ids][None] - tile_cost) / epsilon
            highest = jnp.max(scores, axis=(1, 2))
            return highest + jnp.log(jnp.sum(jnp.exp(scores - highest[:, None, None]), axis=(1, 2)))
        return lax.map(one_block, (point_tiles, sq_points, global_ids))

    def atom_sums(point_pot, epsilon):
        def one_block(carry, inputs):
            acc_upper, acc_total = carry
            point_tile, sq_tile, chosen_ids, pot_tile, logw_tile = inputs
            tile_cost = tile_costs(point_tile, sq_tile, chosen_ids)
            scores = logw_tile[:, None, None] + (pot_tile[:, None, None] - tile_cost) / epsilon
            highest = jnp.max(scores, axis=0)
            totals = jnp.sum(jnp.exp(scores - highest[None]), axis=0)
            merged = merge_terms((acc_upper[chosen_ids], acc_total[chosen_ids]), (highest, totals))
            return (acc_upper.at[chosen_ids].set(merged[0]), acc_total.at[chosen_ids].set(merged[1])), None
        starting = (jnp.full((atom_blocks, 128), lowest, jnp.float32), jnp.zeros((atom_blocks, 128), jnp.float32))
        (acc_upper, acc_total), _ = lax.scan(one_block, starting, (point_tiles, sq_points, global_ids, point_pot, logw_points))
        return acc_upper, acc_total

    strength = relaxation[0]
    atom_pot = jnp.zeros((atom_blocks, 128), jnp.float32)
    point_pot = jnp.zeros((point_blocks, 128), jnp.float32)
    for iteration in range(ITERS):
        epsilon = epsilons[iteration]
        factor = strength / (strength + epsilon)
        point_pot = -factor * epsilon * point_sums(atom_pot, epsilon)
        acc_upper, acc_total = atom_sums(point_pot, epsilon)
        atom_pot = -factor * epsilon * (acc_upper + jnp.log(acc_total))
    closing = point_sums(atom_pot, epsilons[ITERS - 1])
    log_mass = logw_points + point_pot / epsilons[ITERS - 1] + closing
    return (point_pot.reshape(-1), atom_pot.reshape(-1), log_mass.reshape(-1))
```

```python
import functools
import math

import jax
import jax.numpy as jnp
from jax import lax
from jax.experimental import pallas as pl
from jax.experimental.pallas import tpu as pltpu
from jax.sharding import PartitionSpec as P

MESH = pl.DeviceIdType.MESH
lowest = -1e30
LOG2E = 1.0 / math.log(2.0)
LN2 = math.log(2.0)
GROUP = 4
STRIP = 32


def kernel(
    npts,
    natom,
    kept_h,
    eps_h,
    relax_h,
    points_h,
    atoms_h,
    plogw_h,
    alogw_h,
    pot_out,
    apot_out,
    mass_out,
    kept_s,
    eps_s,
    relax_s,
    plogw,
    pts_v,
    win,
    wlogw,
    x_s,
    spn,
    l2,
    a2,
    krow,
    mrow,
    srow,
    b2,
    san,
    acc,
    part,
    rb,
    lsem,
    hsend,
    hrecv,
    fsend,
    frecv,
    gsend,
    grecv,
    esend,
    erecv,
    near,
    far,
):
    blocks, rows, depth = pts_v.shape
    keep = krow.shape[0] // blocks
    panel = alogw_h.shape[0]
    iters = eps_s.shape[0]
    half = panel // 2
    mine, here = lax.axis_index("pts"), lax.axis_index("atom")
    up, down = lax.rem(here + 1, natom), lax.rem(here + natom - 1, natom)
    core = lax.rem(mine, 2)
    partner = mine + 1 - 2 * core

    local = []
    for n, (src, dst) in enumerate(
        (
            (kept_h, kept_s),
            (plogw_h, plogw),
            (eps_h, eps_s),
            (relax_h, relax_s),
            (alogw_h, wlogw.at[1]),
            (points_h, pts_v),
            (atoms_h, win.at[pl.ds(panel, panel)]),
        )
    ):
        local.append(pltpu.make_async_copy(src, dst, lsem.at[n]))
    for copy in local:
        copy.start()

    partners = []
    for o in (-2, -1, 0, 1, 2):
        for t in range(npts):
            if o == 0 and t == 0:
                continue
            partners.append((o, t))

    def target(o, t):
        return (lax.rem(mine + t, npts), lax.rem(here - o + natom, natom))

    group = [target(0, t) for t in range(1, npts)]
    sides = [(mine, up), (mine, down)]
    barrier = pltpu.get_barrier_semaphore()
    for device in sides + group:
        pl.semaphore_signal(barrier, inc=1, device_id=device, device_id_type=MESH)
    pl.semaphore_wait(barrier, len(sides) + len(group))
    for device in group:
        pl.semaphore_signal(near, inc=1, device_id=device, device_id_type=MESH)

    halo, small = [], []
    mine_half = pl.ds(core * half, half)
    for side, (slot, to) in enumerate(((0, up), (2, down))):
        halo.append(
            pltpu.make_async_remote_copy(
                src_ref=atoms_h.at[mine_half],
                dst_ref=win.at[pl.ds(slot * panel + core * half, half)],
                send_sem=hsend.at[side],
                recv_sem=hrecv.at[side],
                device_id=(mine, to),
                device_id_type=MESH,
            )
        )
        small.append(
            pltpu.make_async_remote_copy(
                src_ref=alogw_h,
                dst_ref=wlogw.at[slot],
                send_sem=gsend.at[side],
                recv_sem=grecv.at[side],
                device_id=(mine, to),
                device_id_type=MESH,
            )
        )
    for copy in halo + small:
        copy.start()

    for copy in local:
        copy.wait()

    def prepare(q, carry):
        p = pts_v[q].astype(jnp.float32)
        sq = jnp.sum(p * p, axis=1, keepdims=True) * (0.5 / depth)
        spn[q] = jnp.broadcast_to(sq, (rows, 128))
        lw = jnp.broadcast_to(plogw[pl.ds(q, 1), :], (rows, 128)) * LOG2E
        l2[q] = jnp.transpose(lw)
        for k in range(keep):
            krow[pl.ds(q * keep + k, 1), :] = jnp.full((1, 128), kept_s[k, q], jnp.int32)
        return carry

    lax.fori_loop(0, blocks, prepare, 0)

    def norms(slot):
        for w in range(slot * panel, (slot + 1) * panel):
            a = win[w].astype(jnp.float32)
            sq = jnp.sum(a * a, axis=1, keepdims=True) * (0.5 / depth)
            san[pl.ds(w, 1), :] = jnp.transpose(jnp.broadcast_to(sq, (rows, 128)))[0:1, :]

    norms(1)
    forward = []
    for side, slot in enumerate((0, 2)):
        halo[side].wait_recv()
        piece = pl.ds(slot * panel + core * half, half)
        forward.append(
            pltpu.make_async_remote_copy(
                src_ref=win.at[piece],
                dst_ref=win.at[piece],
                send_sem=fsend.at[side],
                recv_sem=frecv.at[side],
                device_id=(partner, here),
                device_id_type=MESH,
            )
        )
        forward[side].start()
    for side, slot in enumerate((0, 2)):
        forward[side].wait()
        norms(slot)
    for copy in halo:
        copy.wait_send()
    for copy in small:
        copy.wait()

    pl.semaphore_wait(near, len(group))
    for device in sides:
        pl.semaphore_signal(far, inc=1, device_id=device, device_id_type=MESH)

    strength = relax_s[0]
    lanes = lax.broadcasted_iota(jnp.int32, (rows, 128), 1)
    acc[...] = jnp.zeros_like(acc)

    def bias(inv_eps, j, pot):
        block = pl.ds(j * panel, panel)
        b2[block, :] = LOG2E * (wlogw[j] + (pot - san[block, :]) * inv_eps)

    def point_lse(q, ratio, brow, strip):
        t = x_s[q, strip, :]
        if ratio is not None:
            t = t * ratio
            x_s[q, strip, :] = t
        t = t + brow
        top = jnp.max(t, axis=1, keepdims=True)
        total = jnp.sum(jnp.exp2(t - top), axis=1, keepdims=True)
        return jnp.broadcast_to(top + jnp.log2(total), (STRIP, 128))

    def bias_row(q):
        return jnp.concatenate(
            [b2[pl.ds(kept_s[k, q], 1), :] for k in range(keep)], axis=1
        )

    for it in range(iters):
        eps = eps_s[it]
        inv_eps = jnp.ones((1, 128), jnp.float32) / jnp.full((1, 128), eps, jnp.float32)
        factor = strength / (strength + eps)
        scale = (LOG2E / depth) * inv_eps[0:1, 0:1]
        if it == 0:
            for j in range(3):
                bias(inv_eps, j, jnp.zeros((panel, 128), jnp.float32))
        ratio = None if it == 0 else eps_s[it - 1] * inv_eps[0:1, 0:1]
        last = it == iters - 1

        def one(q):
            if it == 0:
                chosen = jnp.concatenate(
                    [win[kept_s[k, q]] for k in range(keep)], axis=0
                )
                x_s[q] = scale * lax.dot_general(
                    pts_v[q],
                    chosen,
                    (((1,), (1,)), ((), ())),
                    preferred_element_type=jnp.float32,
                )
            brow = bias_row(q)
            for r in range(rows // STRIP):
                strip = pl.ds(r * STRIP, STRIP)
                lse = point_lse(q, ratio, brow, strip)
                sp = spn[q, strip, :]
                pot = factor * (sp - (eps * LN2) * lse)
                a2[q, strip, :] = l2[q, strip, :] + (pot - sp) * (LOG2E * inv_eps)
                if last:
                    acc[strip, :] = jnp.where(lanes[:STRIP] == q, pot, acc[strip, :])
            for k in range(keep):
                u = x_s[q, :, pl.ds(k * 128, 128)] + a2[q]
                top = jnp.max(u, axis=0, keepdims=True)
                total = jnp.sum(jnp.exp2(u - top), axis=0, keepdims=True)
                mrow[pl.ds(q * keep + k, 1), :] = top
                srow[pl.ds(q * keep + k, 1), :] = total

        def step(g, carry):
            for i in range(GROUP):
                one(g * GROUP + i)
            return carry

        lax.fori_loop(0, blocks // GROUP, step, 0)

        member, m = krow[...], mrow[...]
        tops, shift = [], jnp.zeros_like(m)
        for w in range(3 * panel):
            chosen = member == w
            tops.append(jnp.max(jnp.where(chosen, m, lowest), axis=0, keepdims=True))
            shift = jnp.where(chosen, tops[w], shift)
        terms = srow[...] * jnp.exp2(m - shift)
        for w in range(3 * panel):
            total = jnp.sum(jnp.where(member == w, terms, 0.0), axis=0, keepdims=True)
            part[it, w // panel, pl.ds(w % panel, 1), :] = jnp.where(
                total > 0.0, tops[w] + jnp.log2(total), lowest
            )
        rb[it, 2, mine] = part[it]

        copies = []
        for n, (o, t) in enumerate(partners):
            low, high = max(0, -o), min(3, 3 - o)
            copies.append(
                pltpu.make_async_remote_copy(
                    src_ref=part.at[it, pl.ds(low, high - low)],
                    dst_ref=rb.at[it, o + 2, mine, pl.ds(low + o, high - low)],
                    send_sem=esend.at[it, n],
                    recv_sem=erecv.at[it, n],
                    device_id=target(o, t),
                    device_id_type=MESH,
                )
            )
        if it == 0:
            pl.semaphore_wait(far, len(sides))
        for copy in copies:
            copy.start()
        if last:
            pot_out[...] = jnp.transpose(acc[...])[:blocks]
        for copy in copies:
            copy.wait()

        next_eps = eps_s[min(it + 1, iters - 1)]
        next_inv = jnp.ones((1, 128), jnp.float32) / jnp.full((1, 128), next_eps, jnp.float32)
        for j in range(3):
            terms = [
                rb[it, o + 2, s, j] for o in range(j - 2, j + 1) for s in range(npts)
            ]
            top = functools.reduce(jnp.maximum, terms)
            total = functools.reduce(jnp.add, [jnp.exp2(term - top) for term in terms])
            lse = jnp.where(top > 0.5 * lowest, top + jnp.log2(total), -jnp.inf)
            pot = factor * (san[pl.ds(j * panel, panel), :] - (eps * LN2) * lse)
            bias(next_inv, j, pot)
            if last and j == 1:
                apot_out[...] = pot

    def closing(g, carry):
        for i in range(GROUP):
            q = g * GROUP + i
            brow = bias_row(q)
            for r in range(rows // STRIP):
                strip = pl.ds(r * STRIP, STRIP)
                mass = (point_lse(q, None, brow, strip) + a2[q, strip, :]) * LN2
                acc[strip, :] = jnp.where(lanes[:STRIP] == q, mass, acc[strip, :])
        return carry

    lax.fori_loop(0, blocks // GROUP, closing, 0)
    mass_out[...] = jnp.transpose(acc[...])[:blocks]


def finish(pot, apot, mass, pot_out, apot_out, mass_out, sem):
    copies = [
        pltpu.make_async_copy(src, dst, sem.at[n])
        for n, (src, dst) in enumerate(
            ((pot, pot_out), (apot, apot_out), (mass, mass_out))
        )
    ]
    for copy in copies:
        copy.start()
    for copy in copies:
        copy.wait()


def per_device(points, atoms, kept, point_logw, atom_logw, epsilons, relaxation):
    depth = points.shape[1]
    blocks = points.shape[0] // 128
    panel = atoms.shape[0] // 128
    keep = kept.shape[1]
    iters = epsilons.shape[0]
    npts, natom = lax.axis_size("pts"), lax.axis_size("atom")
    partners = 5 * npts - 1
    f32, bf16 = jnp.float32, jnp.bfloat16
    vmem = pl.BlockSpec(memory_space=pltpu.VMEM)
    hbm = pl.BlockSpec(memory_space=pltpu.HBM)
    keep_here = functools.partial(
        pltpu.with_memory_space_constraint, memory_space=pltpu.HBM
    )
    pot, apot, mass = pl.pallas_call(
        functools.partial(kernel, npts, natom),
        out_shape=(
            jax.ShapeDtypeStruct((blocks, 128), f32),
            jax.ShapeDtypeStruct((panel, 128), f32),
            jax.ShapeDtypeStruct((blocks, 128), f32),
        ),
        in_specs=[hbm] * 7,
        out_specs=(vmem, vmem, vmem),
        scratch_shapes=[
            pltpu.SMEM((keep, blocks), jnp.int32),
            pltpu.SMEM((iters,), f32),
            pltpu.SMEM((1,), f32),
            pltpu.VMEM((blocks, 128), f32),
            pltpu.VMEM((blocks, 128, depth), bf16),
            pltpu.VMEM((3 * panel, 128, depth), bf16),
            pltpu.VMEM((3, panel, 128), f32),
            pltpu.VMEM((blocks, 128, keep * 128), f32),
            pltpu.VMEM((blocks, 128, 128), f32),
            pltpu.VMEM((blocks, 128, 128), f32),
            pltpu.VMEM((blocks, 128, 128), f32),
            pltpu.VMEM((blocks * keep, 128), jnp.int32),
            pltpu.VMEM((blocks * keep, 128), f32),
            pltpu.VMEM((blocks * keep, 128), f32),
            pltpu.VMEM((3 * panel, 128), f32),
            pltpu.VMEM((3 * panel, 128), f32),
            pltpu.VMEM((128, 128), f32),
            pltpu.VMEM((iters, 3, panel, 128), f32),
            pltpu.VMEM((iters, 5, npts, 3, panel, 128), f32),
            pltpu.SemaphoreType.DMA((7,)),
            pltpu.SemaphoreType.DMA((2,)),
            pltpu.SemaphoreType.DMA((2,)),
            pltpu.SemaphoreType.DMA((2,)),
            pltpu.SemaphoreType.DMA((2,)),
            pltpu.SemaphoreType.DMA((2,)),
            pltpu.SemaphoreType.DMA((2,)),
            pltpu.SemaphoreType.DMA((iters, partners)),
            pltpu.SemaphoreType.DMA((iters, partners)),
            pltpu.SemaphoreType.REGULAR,
            pltpu.SemaphoreType.REGULAR,
        ],
        compiler_params=pltpu.CompilerParams(
            collective_id=0, has_side_effects=True, vmem_limit_bytes=48 << 20
        ),
    )(
        keep_here(kept.T),
        keep_here(epsilons),
        relaxation,
        keep_here(points.reshape(blocks, 128, depth)),
        keep_here(atoms.reshape(panel, 128, depth)),
        keep_here(point_logw.reshape(blocks, 128)),
        keep_here(atom_logw.reshape(panel, 128)),
    )
    pot, apot, mass = pl.pallas_call(
        finish,
        out_shape=tuple(jax.ShapeDtypeStruct(v.shape, f32) for v in (pot, apot, mass)),
        in_specs=[vmem] * 3,
        out_specs=(hbm,) * 3,
        scratch_shapes=[pltpu.SemaphoreType.DMA((3,))],
        compiler_params=pltpu.CompilerParams(vmem_limit_bytes=48 << 20),
    )(pot, apot, mass)
    return pot.reshape(-1), apot.reshape(-1), mass.reshape(-1)


def solution(mesh):
    return jax.shard_map(
        per_device,
        mesh=mesh,
        in_specs=(
            P(("pts", "atom"), None),
            P("atom", None),
            P(("pts", "atom"), None),
            P(("pts", "atom")),
            P("atom"),
            P(),
            P(),
        ),
        out_specs=(P(("pts", "atom")), P("atom"), P(("pts", "atom"))),
        check_vma=False,
    )
```

```python
import functools
import math

import jax
import jax.numpy as jnp
from jax import lax
from jax.experimental import pallas as pl
from jax.experimental.pallas import tpu as pltpu
from jax.sharding import PartitionSpec as P

MESH = pl.DeviceIdType.MESH
lowest = -1e30
LOG2E = 1.0 / math.log(2.0)
LN2 = math.log(2.0)
STRIP = 32
GROUP = 4


def kernel(
    npts,
    natom,
    kept_h,
    eps_h,
    relax_h,
    points_h,
    atoms_h,
    plogw_h,
    alogw_h,
    pot_out,
    apot_out,
    mass_out,
    kept_s,
    eps_s,
    relax_s,
    plogw,
    pts_v,
    win,
    wlogw,
    x_s,
    base,
    a2,
    spd,
    krow,
    mrow,
    srow,
    b2,
    san,
    acc,
    acc2,
    part,
    rb,
    lsem,
    hsend,
    hrecv,
    fsend,
    frecv,
    gsend,
    grecv,
    esend,
    erecv,
    near,
    far,
):
    blocks, rows, depth = points_h.shape
    keep = kept_h.shape[0]
    panel = alogw_h.shape[0]
    iters = eps_s.shape[0]
    half = panel // 2
    mine, here = lax.axis_index("pts"), lax.axis_index("atom")
    up, down = lax.rem(here + 1, natom), lax.rem(here + natom - 1, natom)
    core = lax.rem(mine, 2)
    partner = mine + 1 - 2 * core

    local = []
    for n, (src, dst) in enumerate(
        (
            (kept_h, kept_s),
            (plogw_h, plogw),
            (eps_h, eps_s),
            (relax_h, relax_s),
            (alogw_h, wlogw.at[1]),
            (points_h, pts_v.at[pl.ds(0, blocks)]),
            (atoms_h, win.at[pl.ds(panel, panel)]),
        )
    ):
        local.append(pltpu.make_async_copy(src, dst, lsem.at[n]))
    for copy in local:
        copy.start()

    partners = []
    for o in (-2, -1, 0, 1, 2):
        for t in range(npts):
            if o == 0 and t == 0:
                continue
            partners.append((o, t))

    def target(o, t):
        return (lax.rem(mine + t, npts), lax.rem(here - o + natom, natom))

    group = [target(0, t) for t in range(1, npts)]
    sides = [(mine, up), (mine, down)]
    barrier = pltpu.get_barrier_semaphore()
    for device in sides + group:
        pl.semaphore_signal(barrier, inc=1, device_id=device, device_id_type=MESH)
    pl.semaphore_wait(barrier, len(sides) + len(group))
    for device in group:
        pl.semaphore_signal(near, inc=1, device_id=device, device_id_type=MESH)

    halo, small = [], []
    mine_half = pl.ds(core * half, half)
    for side, (slot, to) in enumerate(((0, up), (2, down))):
        halo.append(
            pltpu.make_async_remote_copy(
                src_ref=atoms_h.at[mine_half],
                dst_ref=win.at[pl.ds(slot * panel + core * half, half)],
                send_sem=hsend.at[side],
                recv_sem=hrecv.at[side],
                device_id=(mine, to),
                device_id_type=MESH,
            )
        )
        small.append(
            pltpu.make_async_remote_copy(
                src_ref=alogw_h,
                dst_ref=wlogw.at[slot],
                send_sem=gsend.at[side],
                recv_sem=grecv.at[side],
                device_id=(mine, to),
                device_id_type=MESH,
            )
        )
    for copy in halo + small:
        copy.start()

    for copy in local:
        copy.wait()

    lanes = lax.broadcasted_iota(jnp.int32, (rows, 128), 1)
    strength = relax_s[0]
    factors, weights = [], []
    for it in range(iters):
        eps = eps_s[it]
        inv_eps = jnp.ones((1, 128), jnp.float32) / jnp.full((1, 128), eps, jnp.float32)
        factors.append(strength / (strength + eps))
        weights.append((factors[it] - 1.0) * LOG2E * inv_eps)
    acc[...] = jnp.zeros_like(acc)
    acc2[...] = jnp.zeros_like(acc2)

    def prepare(q, carry):
        p = pts_v[q].astype(jnp.float32)
        sq = jnp.sum(p * p, axis=1, keepdims=True) * (0.5 / depth)
        sq = jnp.broadcast_to(sq, (rows, 128))
        lw = jnp.broadcast_to(plogw[pl.ds(q, 1), :], (rows, 128)) * LOG2E
        lw = jnp.transpose(lw)
        for it in range(iters):
            base[it, q] = lw + weights[it] * sq
        acc[...] = jnp.where(lanes == q, sq, acc[...])
        for k in range(keep):
            krow[pl.ds(q * keep + k, 1), :] = jnp.full((1, 128), kept_s[k, q], jnp.int32)
        return carry

    lax.fori_loop(0, blocks, prepare, 0)
    spd[...] = jnp.transpose(acc[...])[:blocks]

    def norms(slot):
        for w in range(slot * panel, (slot + 1) * panel):
            a = win[w].astype(jnp.float32)
            sq = jnp.sum(a * a, axis=1, keepdims=True) * (0.5 / depth)
            san[pl.ds(w, 1), :] = jnp.transpose(jnp.broadcast_to(sq, (rows, 128)))[0:1, :]

    norms(1)
    forward = []
    for side, slot in enumerate((0, 2)):
        halo[side].wait_recv()
        piece = pl.ds(slot * panel + core * half, half)
        forward.append(
            pltpu.make_async_remote_copy(
                src_ref=win.at[piece],
                dst_ref=win.at[piece],
                send_sem=fsend.at[side],
                recv_sem=frecv.at[side],
                device_id=(partner, here),
                device_id_type=MESH,
            )
        )
        forward[side].start()
    for side, slot in enumerate((0, 2)):
        forward[side].wait()
        norms(slot)
    for copy in halo:
        copy.wait_send()
    for copy in small:
        copy.wait()

    pl.semaphore_wait(near, len(group))
    for device in sides:
        pl.semaphore_signal(far, inc=1, device_id=device, device_id_type=MESH)

    def bias(inv_eps, j, pot):
        block = pl.ds(j * panel, panel)
        b2[block, :] = LOG2E * (wlogw[j] + (pot - san[block, :]) * inv_eps)

    def bias_row(q):
        return jnp.concatenate(
            [b2[pl.ds(kept_s[k, q], 1), :] for k in range(keep)], axis=1
        )

    def point_lse(q, brow, strip):
        t = x_s[q, strip, :] + brow
        top = jnp.max(t, axis=1, keepdims=True)
        total = jnp.sum(jnp.exp2(t - top), axis=1, keepdims=True)
        shape = (STRIP, 128)
        return jnp.broadcast_to(top, shape), jnp.broadcast_to(total, shape)

    strips = [pl.ds(r * STRIP, STRIP) for r in range(rows // STRIP)]

    for it in range(iters):
        eps = eps_s[it]
        inv_eps = jnp.ones((1, 128), jnp.float32) / jnp.full((1, 128), eps, jnp.float32)
        factor = factors[it]
        scale = (LOG2E / depth) * inv_eps[0:1, 0:1]
        if it == 0:
            for j in range(3):
                bias(inv_eps, j, jnp.zeros((panel, 128), jnp.float32))
        last = it == iters - 1

        def products(q):
            ids = [kept_s[k, jnp.minimum(q, blocks - 1)] for k in range(keep)]
            chosen = jnp.concatenate([win[w] for w in ids], axis=0)
            x_s[q] = scale * lax.dot_general(
                pts_v[q],
                chosen,
                (((1,), (1,)), ((), ())),
                preferred_element_type=jnp.float32,
            )

        def one(q):
            brow = bias_row(q)
            for strip in strips:
                top, total = point_lse(q, brow, strip)
                a2[q, strip, :] = base[it, q, strip, :] - factor * (
                    top + jnp.log2(total)
                )
            for k in range(keep):
                u = x_s[q, :, pl.ds(k * 128, 128)] + a2[q]
                top = jnp.max(u, axis=0, keepdims=True)
                total = jnp.sum(jnp.exp2(u - top), axis=0, keepdims=True)
                mrow[pl.ds(q * keep + k, 1), :] = top
                srow[pl.ds(q * keep + k, 1), :] = total

        def step(g, carry):
            for i in range(GROUP):
                one(g * GROUP + i)
                if it == 0:
                    products((g + 1) * GROUP + i)
            return carry

        if it == 0:
            for i in range(GROUP):
                products(i)
        lax.fori_loop(0, blocks // GROUP, step, 0)

        member, m = krow[...], mrow[...]
        tops, shift = [], jnp.zeros_like(m)
        for w in range(3 * panel):
            chosen = member == w
            tops.append(jnp.max(jnp.where(chosen, m, lowest), axis=0, keepdims=True))
            shift = jnp.where(chosen, tops[w], shift)
        terms = srow[...] * jnp.exp2(m - shift)
        for w in range(3 * panel):
            total = jnp.sum(jnp.where(member == w, terms, 0.0), axis=0, keepdims=True)
            part[it, w // panel, pl.ds(w % panel, 1), :] = jnp.where(
                total > 0.0, tops[w] + jnp.log2(total), lowest
            )
        rb[it, 2, mine] = part[it]

        copies = []
        for n, (o, t) in enumerate(partners):
            low, high = max(0, -o), min(3, 3 - o)
            copies.append(
                pltpu.make_async_remote_copy(
                    src_ref=part.at[it, pl.ds(low, high - low)],
                    dst_ref=rb.at[it, o + 2, mine, pl.ds(low + o, high - low)],
                    send_sem=esend.at[it, n],
                    recv_sem=erecv.at[it, n],
                    device_id=target(o, t),
                    device_id_type=MESH,
                )
            )
        if it == 0:
            pl.semaphore_wait(far, len(sides))
        for copy in copies:
            copy.start()
        if last:

            def gather(q, carry):
                acc[...] = jnp.where(lanes == q, a2[q], acc[...])
                return carry

            lax.fori_loop(0, blocks, gather, 0)
            dense = jnp.transpose(acc[...])[:blocks]
            pot_out[...] = spd[...] + (dense - LOG2E * plogw[...]) * (eps * LN2)
        else:
            ratio = eps / jnp.full((1, 128), eps_s[it + 1], jnp.float32)[0:1, 0:1]

            def rescale(q, carry):
                x_s[q] = x_s[q] * ratio
                return carry

            lax.fori_loop(0, blocks, rescale, 0)
        for copy in copies:
            copy.wait()

        next_eps = eps_s[min(it + 1, iters - 1)]
        next_inv = jnp.ones((1, 128), jnp.float32) / jnp.full((1, 128), next_eps, jnp.float32)
        for j in range(3):
            terms = [
                rb[it, o + 2, s, j] for o in range(j - 2, j + 1) for s in range(npts)
            ]
            top = functools.reduce(jnp.maximum, terms)
            total = functools.reduce(jnp.add, [jnp.exp2(term - top) for term in terms])
            lse = jnp.where(top > 0.5 * lowest, top + jnp.log2(total), -jnp.inf)
            pot = factor * (san[pl.ds(j * panel, panel), :] - (eps * LN2) * lse)
            bias(next_inv, j, pot)
            if last and j == 1:
                apot_out[...] = pot

    def closing(g, carry):
        for i in range(GROUP):
            q = g * GROUP + i
            brow = bias_row(q)
            for strip in strips:
                top, total = point_lse(q, brow, strip)
                here = lanes[:STRIP] == q
                acc[strip, :] = jnp.where(here, top, acc[strip, :])
                acc2[strip, :] = jnp.where(here, total, acc2[strip, :])
        return carry

    lax.fori_loop(0, blocks // GROUP, closing, 0)
    lse = acc[...] + jnp.log2(acc2[...])
    mass_out[...] = (jnp.transpose(lse)[:blocks] + dense) * LN2


def finish(pot, apot, mass, pot_out, apot_out, mass_out, sem):
    copies = [
        pltpu.make_async_copy(src, dst, sem.at[n])
        for n, (src, dst) in enumerate(
            ((pot, pot_out), (apot, apot_out), (mass, mass_out))
        )
    ]
    for copy in copies:
        copy.start()
    for copy in copies:
        copy.wait()


def per_device(points, atoms, kept, point_logw, atom_logw, epsilons, relaxation):
    depth = points.shape[1]
    blocks = points.shape[0] // 128
    panel = atoms.shape[0] // 128
    keep = kept.shape[1]
    iters = epsilons.shape[0]
    npts, natom = lax.axis_size("pts"), lax.axis_size("atom")
    partners = 5 * npts - 1
    f32, bf16 = jnp.float32, jnp.bfloat16
    vmem = pl.BlockSpec(memory_space=pltpu.VMEM)
    hbm = pl.BlockSpec(memory_space=pltpu.HBM)
    keep_here = functools.partial(
        pltpu.with_memory_space_constraint, memory_space=pltpu.HBM
    )
    pot, apot, mass = pl.pallas_call(
        functools.partial(kernel, npts, natom),
        out_shape=(
            jax.ShapeDtypeStruct((blocks, 128), f32),
            jax.ShapeDtypeStruct((panel, 128), f32),
            jax.ShapeDtypeStruct((blocks, 128), f32),
        ),
        in_specs=[hbm] * 7,
        out_specs=(vmem, vmem, vmem),
        scratch_shapes=[
            pltpu.SMEM((keep, blocks), jnp.int32),
            pltpu.SMEM((iters,), f32),
            pltpu.SMEM((1,), f32),
            pltpu.VMEM((blocks, 128), f32),
            pltpu.VMEM((blocks + GROUP, 128, depth), bf16),
            pltpu.VMEM((3 * panel, 128, depth), bf16),
            pltpu.VMEM((3, panel, 128), f32),
            pltpu.VMEM((blocks + GROUP, 128, keep * 128), f32),
            pltpu.VMEM((iters, blocks, 128, 128), f32),
            pltpu.VMEM((blocks, 128, 128), f32),
            pltpu.VMEM((blocks, 128), f32),
            pltpu.VMEM((blocks * keep, 128), jnp.int32),
            pltpu.VMEM((blocks * keep, 128), f32),
            pltpu.VMEM((blocks * keep, 128), f32),
            pltpu.VMEM((3 * panel, 128), f32),
            pltpu.VMEM((3 * panel, 128), f32),
            pltpu.VMEM((128, 128), f32),
            pltpu.VMEM((128, 128), f32),
            pltpu.VMEM((iters, 3, panel, 128), f32),
            pltpu.VMEM((iters, 5, npts, 3, panel, 128), f32),
            pltpu.SemaphoreType.DMA((7,)),
            pltpu.SemaphoreType.DMA((2,)),
            pltpu.SemaphoreType.DMA((2,)),
            pltpu.SemaphoreType.DMA((2,)),
            pltpu.SemaphoreType.DMA((2,)),
            pltpu.SemaphoreType.DMA((2,)),
            pltpu.SemaphoreType.DMA((2,)),
            pltpu.SemaphoreType.DMA((iters, partners)),
            pltpu.SemaphoreType.DMA((iters, partners)),
            pltpu.SemaphoreType.REGULAR,
            pltpu.SemaphoreType.REGULAR,
        ],
        compiler_params=pltpu.CompilerParams(
            collective_id=0, has_side_effects=True, vmem_limit_bytes=48 << 20
        ),
    )(
        keep_here(kept.T),
        keep_here(epsilons),
        relaxation,
        keep_here(points.reshape(blocks, 128, depth)),
        keep_here(atoms.reshape(panel, 128, depth)),
        keep_here(point_logw.reshape(blocks, 128)),
        keep_here(atom_logw.reshape(panel, 128)),
    )
    pot, apot, mass = pl.pallas_call(
        finish,
        out_shape=tuple(jax.ShapeDtypeStruct(v.shape, f32) for v in (pot, apot, mass)),
        in_specs=[vmem] * 3,
        out_specs=(hbm,) * 3,
        scratch_shapes=[pltpu.SemaphoreType.DMA((3,))],
        compiler_params=pltpu.CompilerParams(vmem_limit_bytes=48 << 20),
    )(pot, apot, mass)
    return pot.reshape(-1), apot.reshape(-1), mass.reshape(-1)


def solution(mesh):
    return jax.shard_map(
        per_device,
        mesh=mesh,
        in_specs=(
            P(("pts", "atom"), None),
            P("atom", None),
            P(("pts", "atom"), None),
            P(("pts", "atom")),
            P("atom"),
            P(),
            P(),
        ),
        out_specs=(P(("pts", "atom")), P("atom"), P(("pts", "atom"))),
        check_vma=False,
    )
```

```python
import functools
import math

import jax
import jax.numpy as jnp
from jax import lax
from jax.experimental import pallas as pl
from jax.experimental.pallas import tpu as pltpu
from jax.sharding import PartitionSpec as P

MESH = pl.DeviceIdType.MESH
lowest = -1e30
LOG2E = 1.0 / math.log(2.0)
LN2 = math.log(2.0)
STRIP = 32
GROUP = 4


def kernel(
    npts,
    natom,
    kept_h,
    eps_h,
    relax_h,
    points_h,
    atoms_h,
    plogw_h,
    alogw_h,
    pot_out,
    apot_out,
    mass_out,
    kept_s,
    eps_s,
    relax_s,
    plogw,
    pts_v,
    win,
    masses,
    x_s,
    base,
    a2,
    spd,
    krow,
    mrow,
    srow,
    b2,
    acc,
    acc2,
    part,
    rb,
    lsem,
    hsend,
    hrecv,
    fsend,
    frecv,
    gsend,
    grecv,
    esend,
    erecv,
    near,
    far,
):
    blocks, rows, depth = points_h.shape
    keep = kept_h.shape[0]
    panel = alogw_h.shape[0]
    iters = eps_s.shape[0]
    half = panel // 2
    mine, here = lax.axis_index("pts"), lax.axis_index("atom")
    up, down = lax.rem(here + 1, natom), lax.rem(here + natom - 1, natom)
    core = lax.rem(mine, 2)
    odd = lax.rem(here, 2)
    farther = lax.rem(here - 1 + 2 * odd + natom, natom)
    closer = here + 1 - 2 * odd
    partner = mine + 1 - 2 * core

    local = []
    for n, (src, dst) in enumerate(
        (
            (kept_h, kept_s),
            (plogw_h, plogw),
            (eps_h, eps_s),
            (relax_h, relax_s),
            (alogw_h, masses.at[1, 0]),
            (points_h, pts_v.at[pl.ds(0, blocks)]),
            (atoms_h, win.at[pl.ds(panel, panel)]),
        )
    ):
        local.append(pltpu.make_async_copy(src, dst, lsem.at[n]))
    for copy in local:
        copy.start()

    partners = []
    for o in (-2, -1, 0, 1, 2):
        for t in range(npts):
            if o == 0 and t == 0:
                continue
            partners.append((o, t))

    def target(o, t):
        return (lax.rem(mine + t, npts), lax.rem(here - o + natom, natom))

    group = [target(0, t) for t in range(1, npts)]
    sides = [(mine, up), (mine, down)]
    barrier = pltpu.get_barrier_semaphore()
    for device in sides + group:
        pl.semaphore_signal(barrier, inc=1, device_id=device, device_id_type=MESH)
    pl.semaphore_wait(barrier, len(sides) + len(group))
    for device in group:
        pl.semaphore_signal(near, inc=1, device_id=device, device_id_type=MESH)

    halo, small = [], []
    mine_half = pl.ds(core * half, half)
    for side, (slot, to) in enumerate(((2 - 2 * odd, farther), (2 * odd, closer))):
        halo.append(
            pltpu.make_async_remote_copy(
                src_ref=atoms_h.at[mine_half],
                dst_ref=win.at[pl.ds(slot * panel + core * half, half)],
                send_sem=hsend.at[side],
                recv_sem=hrecv.at[side],
                device_id=(mine, to),
                device_id_type=MESH,
            )
        )
        small.append(
            pltpu.make_async_remote_copy(
                src_ref=masses.at[1],
                dst_ref=masses.at[slot],
                send_sem=gsend.at[side],
                recv_sem=grecv.at[side],
                device_id=(mine, to),
                device_id_type=MESH,
            )
        )
    for copy in halo:
        copy.start()

    for copy in local:
        copy.wait()

    for w in range(panel):
        a = win[panel + w].astype(jnp.float32)
        sq = jnp.sum(a * a, axis=1, keepdims=True) * (0.5 / depth)
        masses[1, 1, pl.ds(w, 1), :] = jnp.transpose(
            jnp.broadcast_to(sq, (rows, 128))
        )[0:1, :]
    for copy in small:
        copy.start()

    lanes = lax.broadcasted_iota(jnp.int32, (rows, 128), 1)
    strength = relax_s[0]
    factors, weights = [], []
    for it in range(iters):
        eps = eps_s[it]
        inv_eps = jnp.ones((1, 128), jnp.float32) / jnp.full((1, 128), eps, jnp.float32)
        factors.append(strength / (strength + eps))
        weights.append((factors[it] - 1.0) * LOG2E * inv_eps)
    acc[...] = jnp.zeros_like(acc)
    acc2[...] = jnp.zeros_like(acc2)

    def prepare(g, carry):
        for i in range(GROUP):
            q = g * GROUP + i
            p = pts_v[q].astype(jnp.float32)
            sq = jnp.sum(p * p, axis=1, keepdims=True) * (0.5 / depth)
            sq = jnp.broadcast_to(sq, (rows, 128))
            lw = jnp.broadcast_to(plogw[pl.ds(q, 1), :], (rows, 128)) * LOG2E
            lw = jnp.transpose(lw)
            for it in range(iters):
                base[it, q] = lw + weights[it] * sq
            acc[...] = jnp.where(lanes == q, sq, acc[...])
            for k in range(keep):
                krow[pl.ds(q * keep + k, 1), :] = jnp.full(
                    (1, 128), kept_s[k, q], jnp.int32
                )
        return carry

    lax.fori_loop(0, blocks // GROUP, prepare, 0)
    spd[...] = jnp.transpose(acc[...])[:blocks]

    forward = []
    for side, slot in enumerate((2 * odd, 2 - 2 * odd)):
        halo[side].wait_recv()
        piece = pl.ds(slot * panel + core * half, half)
        forward.append(
            pltpu.make_async_remote_copy(
                src_ref=win.at[piece],
                dst_ref=win.at[piece],
                send_sem=fsend.at[side],
                recv_sem=frecv.at[side],
                device_id=(partner, here),
                device_id_type=MESH,
            )
        )
        forward[side].start()
    for side in range(2):
        forward[side].wait()
    for copy in halo:
        copy.wait_send()
    for copy in small:
        copy.wait()

    pl.semaphore_wait(near, len(group))
    for device in sides:
        pl.semaphore_signal(far, inc=1, device_id=device, device_id_type=MESH)

    def bias(inv_eps, j, pot):
        block = pl.ds(j * panel, panel)
        b2[block, :] = LOG2E * (masses[j, 0] + (pot - masses[j, 1]) * inv_eps)

    def bias_row(q):
        return jnp.concatenate(
            [b2[pl.ds(kept_s[k, q], 1), :] for k in range(keep)], axis=1
        )

    def point_lse(q, brow, strip):
        t = x_s[q, strip, :] + brow
        top = jnp.max(t, axis=1, keepdims=True)
        total = jnp.sum(jnp.exp2(t - top), axis=1, keepdims=True)
        shape = (STRIP, 128)
        return jnp.broadcast_to(top, shape), jnp.broadcast_to(total, shape)

    strips = [pl.ds(r * STRIP, STRIP) for r in range(rows // STRIP)]

    for it in range(iters):
        eps = eps_s[it]
        inv_eps = jnp.ones((1, 128), jnp.float32) / jnp.full((1, 128), eps, jnp.float32)
        factor = factors[it]
        scale = (LOG2E / depth) * inv_eps[0:1, 0:1]
        if it == 0:
            for j in range(3):
                bias(inv_eps, j, jnp.zeros((panel, 128), jnp.float32))
        last = it == iters - 1

        def products(q):
            ids = [kept_s[k, jnp.minimum(q, blocks - 1)] for k in range(keep)]
            chosen = jnp.concatenate([win[w] for w in ids], axis=0)
            x_s[q] = scale * lax.dot_general(
                pts_v[q],
                chosen,
                (((1,), (1,)), ((), ())),
                preferred_element_type=jnp.float32,
            )

        def one(q):
            brow = bias_row(q)
            for strip in strips:
                top, total = point_lse(q, brow, strip)
                a2[q, strip, :] = base[it, q, strip, :] - factor * (
                    top + jnp.log2(total)
                )
            for k in range(keep):
                u = x_s[q, :, pl.ds(k * 128, 128)] + a2[q]
                top = jnp.max(u, axis=0, keepdims=True)
                total = jnp.sum(jnp.exp2(u - top), axis=0, keepdims=True)
                mrow[pl.ds(q * keep + k, 1), :] = top
                srow[pl.ds(q * keep + k, 1), :] = total

        def step(g, carry):
            for i in range(GROUP):
                one(g * GROUP + i)
                if it == 0:
                    products((g + 1) * GROUP + i)
            return carry

        if it == 0:
            for i in range(GROUP):
                products(i)
        lax.fori_loop(0, blocks // GROUP, step, 0)

        member, m = krow[...], mrow[...]
        tops, shift = [], jnp.zeros_like(m)
        for w in range(3 * panel):
            chosen = member == w
            tops.append(jnp.max(jnp.where(chosen, m, lowest), axis=0, keepdims=True))
            shift = jnp.where(chosen, tops[w], shift)
        terms = srow[...] * jnp.exp2(m - shift)
        for w in range(3 * panel):
            total = jnp.sum(jnp.where(member == w, terms, 0.0), axis=0, keepdims=True)
            part[it, w // panel, pl.ds(w % panel, 1), :] = jnp.where(
                total > 0.0, tops[w] + jnp.log2(total), lowest
            )
        rb[it, 2, mine] = part[it]

        copies = []
        for n, (o, t) in enumerate(partners):
            low, high = max(0, -o), min(3, 3 - o)
            copies.append(
                pltpu.make_async_remote_copy(
                    src_ref=part.at[it, pl.ds(low, high - low)],
                    dst_ref=rb.at[it, o + 2, mine, pl.ds(low + o, high - low)],
                    send_sem=esend.at[it, n],
                    recv_sem=erecv.at[it, n],
                    device_id=target(o, t),
                    device_id_type=MESH,
                )
            )
        if it == 0:
            pl.semaphore_wait(far, len(sides))
        for copy in copies:
            copy.start()
        if last:

            def gather(q, carry):
                acc[...] = jnp.where(lanes == q, a2[q], acc[...])
                return carry

            lax.fori_loop(0, blocks, gather, 0)
            dense = jnp.transpose(acc[...])[:blocks]
            pot_out[...] = spd[...] + (dense - LOG2E * plogw[...]) * (eps * LN2)
        else:
            ratio = eps / jnp.full((1, 128), eps_s[it + 1], jnp.float32)[0:1, 0:1]

            def rescale(q, carry):
                x_s[q] = x_s[q] * ratio
                return carry

            lax.fori_loop(0, blocks, rescale, 0)
        for copy in copies:
            copy.wait()

        next_eps = eps_s[min(it + 1, iters - 1)]
        next_inv = jnp.ones((1, 128), jnp.float32) / jnp.full((1, 128), next_eps, jnp.float32)
        for j in range(3):
            terms = [
                rb[it, o + 2, s, j] for o in range(j - 2, j + 1) for s in range(npts)
            ]
            top = functools.reduce(jnp.maximum, terms)
            total = functools.reduce(jnp.add, [jnp.exp2(term - top) for term in terms])
            lse = jnp.where(top > 0.5 * lowest, top + jnp.log2(total), -jnp.inf)
            pot = factor * (masses[j, 1] - (eps * LN2) * lse)
            bias(next_inv, j, pot)
            if last and j == 1:
                apot_out[...] = pot

    def closing(g, carry):
        for i in range(GROUP):
            q = g * GROUP + i
            brow = bias_row(q)
            for strip in strips:
                top, total = point_lse(q, brow, strip)
                here = lanes[:STRIP] == q
                acc[strip, :] = jnp.where(here, top, acc[strip, :])
                acc2[strip, :] = jnp.where(here, total, acc2[strip, :])
        return carry

    lax.fori_loop(0, blocks // GROUP, closing, 0)
    lse = acc[...] + jnp.log2(acc2[...])
    mass_out[...] = (jnp.transpose(lse)[:blocks] + dense) * LN2


def finish(pot, apot, mass, pot_out, apot_out, mass_out, sem):
    copies = [
        pltpu.make_async_copy(src, dst, sem.at[n])
        for n, (src, dst) in enumerate(
            ((pot, pot_out), (apot, apot_out), (mass, mass_out))
        )
    ]
    for copy in copies:
        copy.start()
    for copy in copies:
        copy.wait()


def per_device(points, atoms, kept, point_logw, atom_logw, epsilons, relaxation):
    depth = points.shape[1]
    blocks = points.shape[0] // 128
    panel = atoms.shape[0] // 128
    keep = kept.shape[1]
    iters = epsilons.shape[0]
    npts, natom = lax.axis_size("pts"), lax.axis_size("atom")
    partners = 5 * npts - 1
    f32, bf16 = jnp.float32, jnp.bfloat16
    vmem = pl.BlockSpec(memory_space=pltpu.VMEM)
    hbm = pl.BlockSpec(memory_space=pltpu.HBM)
    keep_here = functools.partial(
        pltpu.with_memory_space_constraint, memory_space=pltpu.HBM
    )
    pot, apot, mass = pl.pallas_call(
        functools.partial(kernel, npts, natom),
        out_shape=(
            jax.ShapeDtypeStruct((blocks, 128), f32),
            jax.ShapeDtypeStruct((panel, 128), f32),
            jax.ShapeDtypeStruct((blocks, 128), f32),
        ),
        in_specs=[hbm] * 7,
        out_specs=(vmem, vmem, vmem),
        scratch_shapes=[
            pltpu.SMEM((keep, blocks), jnp.int32),
            pltpu.SMEM((iters,), f32),
            pltpu.SMEM((1,), f32),
            pltpu.VMEM((blocks, 128), f32),
            pltpu.VMEM((blocks + GROUP, 128, depth), bf16),
            pltpu.VMEM((3 * panel, 128, depth), bf16),
            pltpu.VMEM((3, 2, panel, 128), f32),
            pltpu.VMEM((blocks + GROUP, 128, keep * 128), f32),
            pltpu.VMEM((iters, blocks, 128, 128), f32),
            pltpu.VMEM((blocks, 128, 128), f32),
            pltpu.VMEM((blocks, 128), f32),
            pltpu.VMEM((blocks * keep, 128), jnp.int32),
            pltpu.VMEM((blocks * keep, 128), f32),
            pltpu.VMEM((blocks * keep, 128), f32),
            pltpu.VMEM((3 * panel, 128), f32),
            pltpu.VMEM((128, 128), f32),
            pltpu.VMEM((128, 128), f32),
            pltpu.VMEM((iters, 3, panel, 128), f32),
            pltpu.VMEM((iters, 5, npts, 3, panel, 128), f32),
            pltpu.SemaphoreType.DMA((7,)),
            pltpu.SemaphoreType.DMA((2,)),
            pltpu.SemaphoreType.DMA((2,)),
            pltpu.SemaphoreType.DMA((2,)),
            pltpu.SemaphoreType.DMA((2,)),
            pltpu.SemaphoreType.DMA((2,)),
            pltpu.SemaphoreType.DMA((2,)),
            pltpu.SemaphoreType.DMA((iters, partners)),
            pltpu.SemaphoreType.DMA((iters, partners)),
            pltpu.SemaphoreType.REGULAR,
            pltpu.SemaphoreType.REGULAR,
        ],
        compiler_params=pltpu.CompilerParams(
            collective_id=0, has_side_effects=True, vmem_limit_bytes=48 << 20
        ),
    )(
        keep_here(kept.T),
        keep_here(epsilons),
        relaxation,
        keep_here(points.reshape(blocks, 128, depth)),
        keep_here(atoms.reshape(panel, 128, depth)),
        keep_here(point_logw.reshape(blocks, 128)),
        keep_here(atom_logw.reshape(panel, 128)),
    )
    pot, apot, mass = pl.pallas_call(
        finish,
        out_shape=tuple(jax.ShapeDtypeStruct(v.shape, f32) for v in (pot, apot, mass)),
        in_specs=[vmem] * 3,
        out_specs=(hbm,) * 3,
        scratch_shapes=[pltpu.SemaphoreType.DMA((3,))],
        compiler_params=pltpu.CompilerParams(vmem_limit_bytes=48 << 20),
    )(pot, apot, mass)
    return pot.reshape(-1), apot.reshape(-1), mass.reshape(-1)


def solution(mesh):
    return jax.shard_map(
        per_device,
        mesh=mesh,
        in_specs=(
            P(("pts", "atom"), None),
            P("atom", None),
            P(("pts", "atom"), None),
            P(("pts", "atom")),
            P("atom"),
            P(),
            P(),
        ),
        out_specs=(P(("pts", "atom")), P("atom"), P(("pts", "atom"))),
        check_vma=False,
    )
```

```python
import functools
import math

import jax
import jax.numpy as jnp
from jax import lax
from jax.experimental import pallas as pl
from jax.experimental.pallas import tpu as pltpu
from jax.sharding import PartitionSpec as P

MESH = pl.DeviceIdType.MESH
lowest = -1e30
LOG2E = 1.0 / math.log(2.0)
LN2 = math.log(2.0)
STRIP = 32
GROUP = 4


def kernel(
    npts,
    natom,
    kept_h,
    eps_h,
    relax_h,
    points_h,
    atoms_h,
    plogw_h,
    alogw_h,
    pot_out,
    apot_out,
    mass_out,
    kept_s,
    eps_s,
    relax_s,
    plogw,
    pts_v,
    win,
    masses,
    x_s,
    base,
    a2,
    spd,
    krow,
    mrow,
    srow,
    b2,
    acc,
    acc2,
    part,
    rb,
    lsem,
    hsend,
    hrecv,
    fsend,
    frecv,
    gsend,
    grecv,
    volume,
    esend,
    erecv,
    near,
    far,
):
    blocks, rows, depth = points_h.shape
    keep = kept_h.shape[0]
    panel = alogw_h.shape[0]
    iters = eps_s.shape[0]
    half = panel // 2
    mine, here = lax.axis_index("pts"), lax.axis_index("atom")
    up, down = lax.rem(here + 1, natom), lax.rem(here + natom - 1, natom)
    core = lax.rem(mine, 2)
    odd = lax.rem(here, 2)
    farther = lax.rem(here - 1 + 2 * odd + natom, natom)
    closer = here + 1 - 2 * odd
    partner = mine + 1 - 2 * core

    local = []
    for n, (src, dst) in enumerate(
        (
            (kept_h, kept_s),
            (plogw_h, plogw),
            (eps_h, eps_s),
            (relax_h, relax_s),
            (alogw_h, masses.at[1, 0]),
            (points_h, pts_v.at[pl.ds(0, blocks)]),
            (atoms_h, win.at[pl.ds(panel, panel)]),
        )
    ):
        local.append(pltpu.make_async_copy(src, dst, lsem.at[n]))
    for copy in local:
        copy.start()

    partners = []
    for o in (-2, -1, 0, 1, 2):
        for t in range(npts):
            if o == 0 and t == 0:
                continue
            partners.append((o, t))

    def target(o, t):
        return (lax.rem(mine + t, npts), lax.rem(here - o + natom, natom))

    group = [target(0, t) for t in range(1, npts)]
    sides = [(mine, up), (mine, down)]
    barrier = pltpu.get_barrier_semaphore()
    for device in sides + group:
        pl.semaphore_signal(barrier, inc=1, device_id=device, device_id_type=MESH)
    pl.semaphore_wait(barrier, len(sides) + len(group))
    for device in group:
        pl.semaphore_signal(near, inc=1, device_id=device, device_id_type=MESH)

    halo, small = [], []
    mine_half = pl.ds(core * half, half)
    for side, (slot, to) in enumerate(((2 - 2 * odd, farther), (2 * odd, closer))):
        halo.append(
            pltpu.make_async_remote_copy(
                src_ref=atoms_h.at[mine_half],
                dst_ref=win.at[pl.ds(slot * panel + core * half, half)],
                send_sem=hsend.at[side],
                recv_sem=hrecv.at[side],
                device_id=(mine, to),
                device_id_type=MESH,
            )
        )
        small.append(
            pltpu.make_async_remote_copy(
                src_ref=masses.at[1],
                dst_ref=masses.at[slot],
                send_sem=gsend.at[side],
                recv_sem=grecv.at[side],
                device_id=(mine, to),
                device_id_type=MESH,
            )
        )
    for copy in halo:
        copy.start()

    for copy in local:
        copy.wait()

    for w in range(panel):
        a = win[panel + w].astype(jnp.float32)
        sq = jnp.sum(a * a, axis=1, keepdims=True) * (0.5 / depth)
        masses[1, 1, pl.ds(w, 1), :] = jnp.transpose(
            jnp.broadcast_to(sq, (rows, 128))
        )[0:1, :]
    for copy in small:
        copy.start()

    lanes = lax.broadcasted_iota(jnp.int32, (rows, 128), 1)
    strength = relax_s[0]
    factors, weights = [], []
    for it in range(iters):
        eps = eps_s[it]
        inv_eps = jnp.ones((1, 128), jnp.float32) / jnp.full((1, 128), eps, jnp.float32)
        factors.append(strength / (strength + eps))
        weights.append((factors[it] - 1.0) * LOG2E * inv_eps)
    acc[...] = jnp.zeros_like(acc)
    acc2[...] = jnp.zeros_like(acc2)

    def prepare(g, carry):
        for i in range(GROUP):
            q = g * GROUP + i
            p = pts_v[q].astype(jnp.float32)
            sq = jnp.sum(p * p, axis=1, keepdims=True) * (0.5 / depth)
            sq = jnp.broadcast_to(sq, (rows, 128))
            lw = jnp.broadcast_to(plogw[pl.ds(q, 1), :], (rows, 128)) * LOG2E
            lw = jnp.transpose(lw)
            for it in range(iters):
                base[it, q] = lw + weights[it] * sq
            acc[...] = jnp.where(lanes == q, sq, acc[...])
            for k in range(keep):
                krow[pl.ds(q * keep + k, 1), :] = jnp.full(
                    (1, 128), kept_s[k, q], jnp.int32
                )
        return carry

    lax.fori_loop(0, blocks // GROUP, prepare, 0)
    spd[...] = jnp.transpose(acc[...])[:blocks]

    forward = []
    for side, slot in enumerate((2 * odd, 2 - 2 * odd)):
        halo[side].wait_recv()
        piece = pl.ds(slot * panel + core * half, half)
        forward.append(
            pltpu.make_async_remote_copy(
                src_ref=win.at[piece],
                dst_ref=win.at[piece],
                send_sem=fsend.at[side],
                recv_sem=frecv.at[side],
                device_id=(partner, here),
                device_id_type=MESH,
            )
        )
        forward[side].start()
    for side in range(2):
        forward[side].wait()
    for copy in halo:
        copy.wait_send()
    for copy in small:
        copy.wait()

    pl.semaphore_wait(near, len(group))
    for device in sides:
        pl.semaphore_signal(far, inc=1, device_id=device, device_id_type=MESH)

    def bias(inv_eps, j, pot):
        block = pl.ds(j * panel, panel)
        b2[block, :] = LOG2E * (masses[j, 0] + (pot - masses[j, 1]) * inv_eps)

    def bias_row(q):
        return jnp.concatenate(
            [b2[pl.ds(kept_s[k, q], 1), :] for k in range(keep)], axis=1
        )

    def point_lse(q, brow, strip):
        t = x_s[q, strip, :] + brow
        top = jnp.max(t, axis=1, keepdims=True)
        total = jnp.sum(jnp.exp2(t - top), axis=1, keepdims=True)
        shape = (STRIP, 128)
        return jnp.broadcast_to(top, shape), jnp.broadcast_to(total, shape)

    strips = [pl.ds(r * STRIP, STRIP) for r in range(rows // STRIP)]

    for it in range(iters):
        eps = eps_s[it]
        inv_eps = jnp.ones((1, 128), jnp.float32) / jnp.full((1, 128), eps, jnp.float32)
        factor = factors[it]
        scale = (LOG2E / depth) * inv_eps[0:1, 0:1]
        if it == 0:
            for j in range(3):
                bias(inv_eps, j, jnp.zeros((panel, 128), jnp.float32))
        last = it == iters - 1

        def products(q):
            ids = [kept_s[k, jnp.minimum(q, blocks - 1)] for k in range(keep)]
            chosen = jnp.concatenate([win[w] for w in ids], axis=0)
            x_s[q] = scale * lax.dot_general(
                pts_v[q],
                chosen,
                (((1,), (1,)), ((), ())),
                preferred_element_type=jnp.float32,
            )

        def one(q):
            brow = bias_row(q)
            for strip in strips:
                top, total = point_lse(q, brow, strip)
                a2[q, strip, :] = base[it, q, strip, :] - factor * (
                    top + jnp.log2(total)
                )
            for k in range(keep):
                u = x_s[q, :, pl.ds(k * 128, 128)] + a2[q]
                top = jnp.max(u, axis=0, keepdims=True)
                total = jnp.sum(jnp.exp2(u - top), axis=0, keepdims=True)
                mrow[pl.ds(q * keep + k, 1), :] = top
                srow[pl.ds(q * keep + k, 1), :] = total

        def step(g, carry):
            for i in range(GROUP):
                one(g * GROUP + i)
                if it == 0:
                    products((g + 1) * GROUP + i)
            return carry

        if it == 0:
            for i in range(GROUP):
                products(i)
        lax.fori_loop(0, blocks // GROUP, step, 0)

        member, m = krow[...], mrow[...]
        tops, shift = [], jnp.zeros_like(m)
        for w in range(3 * panel):
            chosen = member == w
            tops.append(jnp.max(jnp.where(chosen, m, lowest), axis=0, keepdims=True))
            shift = jnp.where(chosen, tops[w], shift)
        terms = srow[...] * jnp.exp2(m - shift)
        for w in range(3 * panel):
            total = jnp.sum(jnp.where(member == w, terms, 0.0), axis=0, keepdims=True)
            part[it, w // panel, pl.ds(w % panel, 1), :] = jnp.where(
                total > 0.0, tops[w] + jnp.log2(total), lowest
            )
        rb[it, 2, mine] = part[it]

        copies = []
        for o, t in partners:
            low, high = max(0, -o), min(3, 3 - o)
            copies.append(
                pltpu.make_async_remote_copy(
                    src_ref=part.at[it, pl.ds(low, high - low)],
                    dst_ref=rb.at[it, o + 2, mine, pl.ds(low + o, high - low)],
                    send_sem=esend.at[it],
                    recv_sem=erecv.at[it],
                    device_id=target(o, t),
                    device_id_type=MESH,
                )
            )
        if it == 0:
            pl.semaphore_wait(far, len(sides))
        for copy in copies:
            copy.start()
        if last:

            def gather(q, carry):
                acc[...] = jnp.where(lanes == q, a2[q], acc[...])
                return carry

            lax.fori_loop(0, blocks, gather, 0)
            dense = jnp.transpose(acc[...])[:blocks]
            pot_out[...] = spd[...] + (dense - LOG2E * plogw[...]) * (eps * LN2)
        else:
            ratio = eps / jnp.full((1, 128), eps_s[it + 1], jnp.float32)[0:1, 0:1]

            def rescale(q, carry):
                x_s[q] = x_s[q] * ratio
                return carry

            lax.fori_loop(0, blocks, rescale, 0)
        for sem in (esend, erecv):
            pltpu.make_async_copy(volume, volume, sem.at[it]).wait()

        next_eps = eps_s[min(it + 1, iters - 1)]
        next_inv = jnp.ones((1, 128), jnp.float32) / jnp.full((1, 128), next_eps, jnp.float32)
        for j in range(3):
            terms = [
                rb[it, o + 2, s, j] for o in range(j - 2, j + 1) for s in range(npts)
            ]
            top = functools.reduce(jnp.maximum, terms)
            total = functools.reduce(jnp.add, [jnp.exp2(term - top) for term in terms])
            lse = jnp.where(top > 0.5 * lowest, top + jnp.log2(total), -jnp.inf)
            pot = factor * (masses[j, 1] - (eps * LN2) * lse)
            bias(next_inv, j, pot)
            if last and j == 1:
                apot_out[...] = pot

    def closing(g, carry):
        for i in range(GROUP):
            q = g * GROUP + i
            brow = bias_row(q)
            for strip in strips:
                top, total = point_lse(q, brow, strip)
                here = lanes[:STRIP] == q
                acc[strip, :] = jnp.where(here, top, acc[strip, :])
                acc2[strip, :] = jnp.where(here, total, acc2[strip, :])
        return carry

    lax.fori_loop(0, blocks // GROUP, closing, 0)
    lse = acc[...] + jnp.log2(acc2[...])
    mass_out[...] = (jnp.transpose(lse)[:blocks] + dense) * LN2


def finish(pot, apot, mass, pot_out, apot_out, mass_out, sem):
    copies = [
        pltpu.make_async_copy(src, dst, sem.at[n])
        for n, (src, dst) in enumerate(
            ((pot, pot_out), (apot, apot_out), (mass, mass_out))
        )
    ]
    for copy in copies:
        copy.start()
    for copy in copies:
        copy.wait()


def per_device(points, atoms, kept, point_logw, atom_logw, epsilons, relaxation):
    depth = points.shape[1]
    blocks = points.shape[0] // 128
    panel = atoms.shape[0] // 128
    keep = kept.shape[1]
    iters = epsilons.shape[0]
    npts, natom = lax.axis_size("pts"), lax.axis_size("atom")
    f32, bf16 = jnp.float32, jnp.bfloat16
    vmem = pl.BlockSpec(memory_space=pltpu.VMEM)
    hbm = pl.BlockSpec(memory_space=pltpu.HBM)
    keep_here = functools.partial(
        pltpu.with_memory_space_constraint, memory_space=pltpu.HBM
    )
    pot, apot, mass = pl.pallas_call(
        functools.partial(kernel, npts, natom),
        out_shape=(
            jax.ShapeDtypeStruct((blocks, 128), f32),
            jax.ShapeDtypeStruct((panel, 128), f32),
            jax.ShapeDtypeStruct((blocks, 128), f32),
        ),
        in_specs=[hbm] * 7,
        out_specs=(vmem, vmem, vmem),
        scratch_shapes=[
            pltpu.SMEM((keep, blocks), jnp.int32),
            pltpu.SMEM((iters,), f32),
            pltpu.SMEM((1,), f32),
            pltpu.VMEM((blocks, 128), f32),
            pltpu.VMEM((blocks + GROUP, 128, depth), bf16),
            pltpu.VMEM((3 * panel, 128, depth), bf16),
            pltpu.VMEM((3, 2, panel, 128), f32),
            pltpu.VMEM((blocks + GROUP, 128, keep * 128), f32),
            pltpu.VMEM((iters, blocks, 128, 128), f32),
            pltpu.VMEM((blocks, 128, 128), f32),
            pltpu.VMEM((blocks, 128), f32),
            pltpu.VMEM((blocks * keep, 128), jnp.int32),
            pltpu.VMEM((blocks * keep, 128), f32),
            pltpu.VMEM((blocks * keep, 128), f32),
            pltpu.VMEM((3 * panel, 128), f32),
            pltpu.VMEM((128, 128), f32),
            pltpu.VMEM((128, 128), f32),
            pltpu.VMEM((iters, 3, panel, 128), f32),
            pltpu.VMEM((iters, 5, npts, 3, panel, 128), f32),
            pltpu.SemaphoreType.DMA((7,)),
            pltpu.SemaphoreType.DMA((2,)),
            pltpu.SemaphoreType.DMA((2,)),
            pltpu.SemaphoreType.DMA((2,)),
            pltpu.SemaphoreType.DMA((2,)),
            pltpu.SemaphoreType.DMA((2,)),
            pltpu.SemaphoreType.DMA((2,)),
            pltpu.VMEM((9 * npts - 3, panel, 128), f32),
            pltpu.SemaphoreType.DMA((iters,)),
            pltpu.SemaphoreType.DMA((iters,)),
            pltpu.SemaphoreType.REGULAR,
            pltpu.SemaphoreType.REGULAR,
        ],
        compiler_params=pltpu.CompilerParams(
            collective_id=0, has_side_effects=True, vmem_limit_bytes=48 << 20
        ),
    )(
        keep_here(kept.T),
        keep_here(epsilons),
        relaxation,
        keep_here(points.reshape(blocks, 128, depth)),
        keep_here(atoms.reshape(panel, 128, depth)),
        keep_here(point_logw.reshape(blocks, 128)),
        keep_here(atom_logw.reshape(panel, 128)),
    )
    pot, apot, mass = pl.pallas_call(
        finish,
        out_shape=tuple(jax.ShapeDtypeStruct(v.shape, f32) for v in (pot, apot, mass)),
        in_specs=[vmem] * 3,
        out_specs=(hbm,) * 3,
        scratch_shapes=[pltpu.SemaphoreType.DMA((3,))],
        compiler_params=pltpu.CompilerParams(vmem_limit_bytes=48 << 20),
    )(pot, apot, mass)
    return pot.reshape(-1), apot.reshape(-1), mass.reshape(-1)


def solution(mesh):
    return jax.shard_map(
        per_device,
        mesh=mesh,
        in_specs=(
            P(("pts", "atom"), None),
            P("atom", None),
            P(("pts", "atom"), None),
            P(("pts", "atom")),
            P("atom"),
            P(),
            P(),
        ),
        out_specs=(P(("pts", "atom")), P("atom"), P(("pts", "atom"))),
        check_vma=False,
    )
```

```python
import functools
import math

import jax
import jax.numpy as jnp
from jax import lax
from jax.experimental import pallas as pl
from jax.experimental.pallas import tpu as pltpu
from jax.sharding import PartitionSpec as P

MESH = pl.DeviceIdType.MESH
lowest = -1e30
LOG2E = 1.0 / math.log(2.0)
LN2 = math.log(2.0)
STRIP = 32
GROUP = 4


def kernel(
    npts,
    natom,
    kept_h,
    eps_h,
    relax_h,
    points_h,
    atoms_h,
    plogw_h,
    alogw_h,
    pot_out,
    apot_out,
    mass_out,
    kept_s,
    eps_s,
    relax_s,
    plogw,
    pts_v,
    win,
    masses,
    x_s,
    base,
    a2,
    spd,
    krow,
    mrow,
    srow,
    b2,
    acc,
    acc2,
    part,
    rb,
    lsem,
    hsend,
    hrecv,
    fsend,
    frecv,
    gsend,
    grecv,
    volume,
    esend,
    erecv,
    near,
    far,
):
    blocks, rows, depth = points_h.shape
    keep = kept_h.shape[0]
    panel = alogw_h.shape[0]
    iters = eps_s.shape[0]
    half = panel // 2
    mine, here = lax.axis_index("pts"), lax.axis_index("atom")
    up, down = lax.rem(here + 1, natom), lax.rem(here + natom - 1, natom)
    core = lax.rem(mine, 2)
    odd = lax.rem(here, 2)
    farther = lax.rem(here - 1 + 2 * odd + natom, natom)
    closer = here + 1 - 2 * odd
    partner = mine + 1 - 2 * core

    local = []
    for n, (src, dst) in enumerate(
        (
            (kept_h, kept_s),
            (plogw_h, plogw),
            (eps_h, eps_s),
            (relax_h, relax_s),
            (alogw_h, masses.at[1, 0]),
            (points_h, pts_v.at[pl.ds(0, blocks)]),
            (atoms_h, win.at[pl.ds(panel, panel)]),
        )
    ):
        local.append(pltpu.make_async_copy(src, dst, lsem.at[n]))
    for copy in local:
        copy.start()

    partners = []
    for o in (-2, 2, -1, 1, 0):
        for t in range(npts):
            if o == 0 and t == 0:
                continue
            partners.append((o, t))

    def target(o, t):
        return (lax.rem(mine + t, npts), lax.rem(here - o + natom, natom))

    group = [target(0, t) for t in range(1, npts)]
    sides = [(mine, up), (mine, down)]
    barrier = pltpu.get_barrier_semaphore()
    for device in sides + group:
        pl.semaphore_signal(barrier, inc=1, device_id=device, device_id_type=MESH)
    pl.semaphore_wait(barrier, len(sides) + len(group))
    for device in group:
        pl.semaphore_signal(near, inc=1, device_id=device, device_id_type=MESH)

    halo, small = [], []
    mine_half = pl.ds(core * half, half)
    for side, (slot, to) in enumerate(((2 - 2 * odd, farther), (2 * odd, closer))):
        halo.append(
            pltpu.make_async_remote_copy(
                src_ref=atoms_h.at[mine_half],
                dst_ref=win.at[pl.ds(slot * panel + core * half, half)],
                send_sem=hsend.at[side],
                recv_sem=hrecv.at[side],
                device_id=(mine, to),
                device_id_type=MESH,
            )
        )
        small.append(
            pltpu.make_async_remote_copy(
                src_ref=masses.at[1],
                dst_ref=masses.at[slot],
                send_sem=gsend.at[side],
                recv_sem=grecv.at[side],
                device_id=(mine, to),
                device_id_type=MESH,
            )
        )
    for copy in halo:
        copy.start()

    for copy in local:
        copy.wait()

    for w in range(panel):
        a = win[panel + w].astype(jnp.float32)
        sq = jnp.sum(a * a, axis=1, keepdims=True) * (0.5 / depth)
        masses[1, 1, pl.ds(w, 1), :] = jnp.transpose(
            jnp.broadcast_to(sq, (rows, 128))
        )[0:1, :]
    for copy in small:
        copy.start()

    lanes = lax.broadcasted_iota(jnp.int32, (rows, 128), 1)
    strength = relax_s[0]
    factors, weights = [], []
    for it in range(iters):
        eps = eps_s[it]
        inv_eps = jnp.ones((1, 128), jnp.float32) / jnp.full((1, 128), eps, jnp.float32)
        factors.append(strength / (strength + eps))
        weights.append((factors[it] - 1.0) * LOG2E * inv_eps)
    acc[...] = jnp.zeros_like(acc)
    acc2[...] = jnp.zeros_like(acc2)

    def prepare(g, carry):
        for i in range(GROUP):
            q = g * GROUP + i
            p = pts_v[q].astype(jnp.float32)
            sq = jnp.sum(p * p, axis=1, keepdims=True) * (0.5 / depth)
            sq = jnp.broadcast_to(sq, (rows, 128))
            lw = jnp.broadcast_to(plogw[pl.ds(q, 1), :], (rows, 128)) * LOG2E
            lw = jnp.transpose(lw)
            for it in range(iters):
                base[it, q] = lw + weights[it] * sq
            acc[...] = jnp.where(lanes == q, sq, acc[...])
            for k in range(keep):
                krow[pl.ds(q * keep + k, 1), :] = jnp.full(
                    (1, 128), kept_s[k, q], jnp.int32
                )
        return carry

    lax.fori_loop(0, blocks // GROUP, prepare, 0)
    spd[...] = jnp.transpose(acc[...])[:blocks]

    forward = []
    for side, slot in enumerate((2 * odd, 2 - 2 * odd)):
        halo[side].wait_recv()
        piece = pl.ds(slot * panel + core * half, half)
        forward.append(
            pltpu.make_async_remote_copy(
                src_ref=win.at[piece],
                dst_ref=win.at[piece],
                send_sem=fsend.at[side],
                recv_sem=frecv.at[side],
                device_id=(partner, here),
                device_id_type=MESH,
            )
        )
        forward[side].start()
    for side in range(2):
        forward[side].wait()
    for copy in halo:
        copy.wait_send()
    for copy in small:
        copy.wait()

    pl.semaphore_wait(near, len(group))
    for device in sides:
        pl.semaphore_signal(far, inc=1, device_id=device, device_id_type=MESH)

    def bias(inv_eps, j, pot):
        block = pl.ds(j * panel, panel)
        b2[block, :] = LOG2E * (masses[j, 0] + (pot - masses[j, 1]) * inv_eps)

    def bias_row(q):
        return jnp.concatenate(
            [b2[pl.ds(kept_s[k, q], 1), :] for k in range(keep)], axis=1
        )

    def point_lse(q, brow, strip):
        t = x_s[q, strip, :] + brow
        top = jnp.max(t, axis=1, keepdims=True)
        total = jnp.sum(jnp.exp2(t - top), axis=1, keepdims=True)
        shape = (STRIP, 128)
        return jnp.broadcast_to(top, shape), jnp.broadcast_to(total, shape)

    strips = [pl.ds(r * STRIP, STRIP) for r in range(rows // STRIP)]

    for it in range(iters):
        eps = eps_s[it]
        inv_eps = jnp.ones((1, 128), jnp.float32) / jnp.full((1, 128), eps, jnp.float32)
        factor = factors[it]
        scale = (LOG2E / depth) * inv_eps[0:1, 0:1]
        if it == 0:
            for j in range(3):
                bias(inv_eps, j, jnp.zeros((panel, 128), jnp.float32))
        last = it == iters - 1

        def products(q):
            ids = [kept_s[k, jnp.minimum(q, blocks - 1)] for k in range(keep)]
            chosen = jnp.concatenate([win[w] for w in ids], axis=0)
            x_s[q] = scale * lax.dot_general(
                pts_v[q],
                chosen,
                (((1,), (1,)), ((), ())),
                preferred_element_type=jnp.float32,
            )

        def one(q):
            brow = bias_row(q)
            for strip in strips:
                top, total = point_lse(q, brow, strip)
                a2[q, strip, :] = base[it, q, strip, :] - factor * (
                    top + jnp.log2(total)
                )
            for k in range(keep):
                u = x_s[q, :, pl.ds(k * 128, 128)] + a2[q]
                top = jnp.max(u, axis=0, keepdims=True)
                total = jnp.sum(jnp.exp2(u - top), axis=0, keepdims=True)
                mrow[pl.ds(q * keep + k, 1), :] = top
                srow[pl.ds(q * keep + k, 1), :] = total

        def step(g, carry):
            for i in range(GROUP):
                one(g * GROUP + i)
                if it == 0:
                    products((g + 1) * GROUP + i)
            return carry

        if it == 0:
            for i in range(GROUP):
                products(i)
        lax.fori_loop(0, blocks // GROUP, step, 0)

        member, m = krow[...], mrow[...]
        tops, shift = [], jnp.zeros_like(m)
        for w in range(3 * panel):
            chosen = member == w
            tops.append(jnp.max(jnp.where(chosen, m, lowest), axis=0, keepdims=True))
            shift = jnp.where(chosen, tops[w], shift)
        terms = srow[...] * jnp.exp2(m - shift)
        for w in range(3 * panel):
            total = jnp.sum(jnp.where(member == w, terms, 0.0), axis=0, keepdims=True)
            part[it, w // panel, pl.ds(w % panel, 1), :] = jnp.where(
                total > 0.0, tops[w] + jnp.log2(total), lowest
            )
        rb[it, 2, mine] = part[it]

        copies = []
        for o, t in partners:
            low, high = max(0, -o), min(3, 3 - o)
            copies.append(
                pltpu.make_async_remote_copy(
                    src_ref=part.at[it, pl.ds(low, high - low)],
                    dst_ref=rb.at[it, o + 2, mine, pl.ds(low + o, high - low)],
                    send_sem=esend.at[it],
                    recv_sem=erecv.at[it],
                    device_id=target(o, t),
                    device_id_type=MESH,
                )
            )
        if it == 0:
            pl.semaphore_wait(far, len(sides))
        for copy in copies:
            copy.start()
        if last:

            def gather(q, carry):
                acc[...] = jnp.where(lanes == q, a2[q], acc[...])
                return carry

            lax.fori_loop(0, blocks, gather, 0)
            dense = jnp.transpose(acc[...])[:blocks]
            pot_out[...] = spd[...] + (dense - LOG2E * plogw[...]) * (eps * LN2)
        else:
            ratio = eps / jnp.full((1, 128), eps_s[it + 1], jnp.float32)[0:1, 0:1]

            def rescale(q, carry):
                x_s[q] = x_s[q] * ratio
                return carry

            lax.fori_loop(0, blocks, rescale, 0)
        for sem in (esend, erecv):
            pltpu.make_async_copy(volume, volume, sem.at[it]).wait()

        next_eps = eps_s[min(it + 1, iters - 1)]
        next_inv = jnp.ones((1, 128), jnp.float32) / jnp.full((1, 128), next_eps, jnp.float32)
        for j in range(3):
            terms = [
                rb[it, o + 2, s, j] for o in range(j - 2, j + 1) for s in range(npts)
            ]
            top = functools.reduce(jnp.maximum, terms)
            total = functools.reduce(jnp.add, [jnp.exp2(term - top) for term in terms])
            lse = jnp.where(top > 0.5 * lowest, top + jnp.log2(total), -jnp.inf)
            pot = factor * (masses[j, 1] - (eps * LN2) * lse)
            bias(next_inv, j, pot)
            if last and j == 1:
                apot_out[...] = pot

    def closing(g, carry):
        for i in range(GROUP):
            q = g * GROUP + i
            brow = bias_row(q)
            for strip in strips:
                top, total = point_lse(q, brow, strip)
                here = lanes[:STRIP] == q
                acc[strip, :] = jnp.where(here, top, acc[strip, :])
                acc2[strip, :] = jnp.where(here, total, acc2[strip, :])
        return carry

    lax.fori_loop(0, blocks // GROUP, closing, 0)
    lse = acc[...] + jnp.log2(acc2[...])
    mass_out[...] = (jnp.transpose(lse)[:blocks] + dense) * LN2


def finish(pot, apot, mass, pot_out, apot_out, mass_out, sem):
    copies = [
        pltpu.make_async_copy(src, dst, sem.at[n])
        for n, (src, dst) in enumerate(
            ((pot, pot_out), (apot, apot_out), (mass, mass_out))
        )
    ]
    for copy in copies:
        copy.start()
    for copy in copies:
        copy.wait()


def per_device(points, atoms, kept, point_logw, atom_logw, epsilons, relaxation):
    depth = points.shape[1]
    blocks = points.shape[0] // 128
    panel = atoms.shape[0] // 128
    keep = kept.shape[1]
    iters = epsilons.shape[0]
    npts, natom = lax.axis_size("pts"), lax.axis_size("atom")
    f32, bf16 = jnp.float32, jnp.bfloat16
    vmem = pl.BlockSpec(memory_space=pltpu.VMEM)
    hbm = pl.BlockSpec(memory_space=pltpu.HBM)
    keep_here = functools.partial(
        pltpu.with_memory_space_constraint, memory_space=pltpu.HBM
    )
    pot, apot, mass = pl.pallas_call(
        functools.partial(kernel, npts, natom),
        out_shape=(
            jax.ShapeDtypeStruct((blocks, 128), f32),
            jax.ShapeDtypeStruct((panel, 128), f32),
            jax.ShapeDtypeStruct((blocks, 128), f32),
        ),
        in_specs=[hbm] * 7,
        out_specs=(vmem, vmem, vmem),
        scratch_shapes=[
            pltpu.SMEM((keep, blocks), jnp.int32),
            pltpu.SMEM((iters,), f32),
            pltpu.SMEM((1,), f32),
            pltpu.VMEM((blocks, 128), f32),
            pltpu.VMEM((blocks + GROUP, 128, depth), bf16),
            pltpu.VMEM((3 * panel, 128, depth), bf16),
            pltpu.VMEM((3, 2, panel, 128), f32),
            pltpu.VMEM((blocks + GROUP, 128, keep * 128), f32),
            pltpu.VMEM((iters, blocks, 128, 128), f32),
            pltpu.VMEM((blocks, 128, 128), f32),
            pltpu.VMEM((blocks, 128), f32),
            pltpu.VMEM((blocks * keep, 128), jnp.int32),
            pltpu.VMEM((blocks * keep, 128), f32),
            pltpu.VMEM((blocks * keep, 128), f32),
            pltpu.VMEM((3 * panel, 128), f32),
            pltpu.VMEM((128, 128), f32),
            pltpu.VMEM((128, 128), f32),
            pltpu.VMEM((iters, 3, panel, 128), f32),
            pltpu.VMEM((iters, 5, npts, 3, panel, 128), f32),
            pltpu.SemaphoreType.DMA((7,)),
            pltpu.SemaphoreType.DMA((2,)),
            pltpu.SemaphoreType.DMA((2,)),
            pltpu.SemaphoreType.DMA((2,)),
            pltpu.SemaphoreType.DMA((2,)),
            pltpu.SemaphoreType.DMA((2,)),
            pltpu.SemaphoreType.DMA((2,)),
            pltpu.VMEM((9 * npts - 3, panel, 128), f32),
            pltpu.SemaphoreType.DMA((iters,)),
            pltpu.SemaphoreType.DMA((iters,)),
            pltpu.SemaphoreType.REGULAR,
            pltpu.SemaphoreType.REGULAR,
        ],
        compiler_params=pltpu.CompilerParams(
            collective_id=0, has_side_effects=True, vmem_limit_bytes=48 << 20
        ),
    )(
        keep_here(kept.T),
        keep_here(epsilons),
        relaxation,
        keep_here(points.reshape(blocks, 128, depth)),
        keep_here(atoms.reshape(panel, 128, depth)),
        keep_here(point_logw.reshape(blocks, 128)),
        keep_here(atom_logw.reshape(panel, 128)),
    )
    pot, apot, mass = pl.pallas_call(
        finish,
        out_shape=tuple(jax.ShapeDtypeStruct(v.shape, f32) for v in (pot, apot, mass)),
        in_specs=[vmem] * 3,
        out_specs=(hbm,) * 3,
        scratch_shapes=[pltpu.SemaphoreType.DMA((3,))],
        compiler_params=pltpu.CompilerParams(vmem_limit_bytes=48 << 20),
    )(pot, apot, mass)
    return pot.reshape(-1), apot.reshape(-1), mass.reshape(-1)


def solution(mesh):
    return jax.shard_map(
        per_device,
        mesh=mesh,
        in_specs=(
            P(("pts", "atom"), None),
            P("atom", None),
            P(("pts", "atom"), None),
            P(("pts", "atom")),
            P("atom"),
            P(),
            P(),
        ),
        out_specs=(P(("pts", "atom")), P("atom"), P(("pts", "atom"))),
        check_vma=False,
    )
```
